32 devices in a mesh: fsdp: 4 (over y, x), ctx: 4 (over z), tp: 2 (over core).
Axes of the slice: x: 2, y: 2, z: 4, core: 2. Of those that a mesh axis runs over, the one named last changes fastest.
Arguments:
- tokens: bfloat16 [2, 2, 4, 128, 2304], P(None, None, 'ctx', 'fsdp'), may hold values from -6 to 6
- segments: int32 [2, 2, 4, 128], P(None, None, 'ctx', 'fsdp'), may hold values from 0 to 3, as said below
- stretch_order: int32 [4], replicated, may hold values from 0 to 3, as said below
- norm_gains: float32 [4, 2304], replicated, may hold values from 0.25 to 1.75
- query_proj: bfloat16 [2304, 2048], P('fsdp', 'tp'), may hold values from -0.125 to 0.125
- keyval_proj: bfloat16 [2304, 2, 1024], P('fsdp', None, 'tp'), may hold values from -0.125 to 0.125
- attn_proj: bfloat16 [2304, 2048], P('fsdp', 'tp'), may hold values from -0.125 to 0.125
- ffn_in: bfloat16 [2304, 2, 9216], P('fsdp', None, 'tp'), may hold values from -0.125 to 0.125
- ffn_out: bfloat16 [2304, 9216], P('fsdp', 'tp'), may hold values from -0.0625 to 0.0625
- cotangent: bfloat16 [2, 2, 4, 128, 2304], P(None, None, 'ctx', 'fsdp'), may hold values from -6 to 6
Outputs:
- result: bfloat16 [2, 2, 4, 128, 2304], P(None, None, 'ctx', 'fsdp')
- grad_tokens: float32 [2, 2, 4, 128, 2304], P(None, None, 'ctx', 'fsdp')
- grad_gains: float32 [4, 2304], replicated
- grad_query: float32 [2304, 2048], P('fsdp', 'tp')
- grad_keyval: float32 [2304, 2, 1024], P('fsdp', None, 'tp')
- grad_attn: float32 [2304, 2048], P('fsdp', 'tp')
- grad_ffn_in: float32 [2304, 2, 9216], P('fsdp', None, 'tp')
- grad_ffn_out: float32 [2304, 9216], P('fsdp', 'tp')
The draws below stay inside these ranges and needn't reach their ends.
Inputs may be any that keep to these rules, and one draw needn't show every extreme that they name: `segments`: along the positions of a sequence the segment ids never fall; every sequence holds exactly four documents, ids 0 to 3. Each of 0 to 3 once; slot c holds position blocks stretch_order[c] and 7 - stretch_order[c] of every sequence.
All inputs are finite; a program needn't handle non-finite values.
Results may differ from the reference program's by a relative error of at most 0.015.
Values may be sent and summed in bfloat16 or wider, within the bound.
No kernel may reach another device: no remote copies, remote signals or barrier semaphores. Data moves between devices by JAX's collectives and lax.ppermute only.
A program may use at most 640 MiB of HBM per device.

```python
import math
import jax
import jax.numpy as jnp
from jax import lax

D = 2304
HEADS = 8
KV_HEADS = 4
HEAD_DIM = 256
FF = 9216
SEQS = 2
HALF_STRETCH = 128
LENGTH = 1024
N_CTX = 4


def document_flags(seq_key):
    cuts = jax.random.permutation(seq_key, LENGTH - 1)[:3].astype(jnp.int32) + 1
    places = jnp.arange(LENGTH, dtype=jnp.int32)
    return jnp.sum(jnp.where(places[None, :] == cuts[:, None], 1, 0), axis=0).astype(jnp.int32)


def layout_tables(key):
    order = jax.random.permutation(jax.random.fold_in(key, 101), N_CTX).astype(jnp.int32)
    seq_keys = jax.random.split(jax.random.fold_in(key, 102), SEQS)
    flags = jax.vmap(document_flags)(seq_keys)
    doc_ids = jnp.cumsum(flags, axis=1).astype(jnp.int32)
    halves = jnp.arange(2, dtype=jnp.int32)[:, None]
    placed = jnp.where(halves == 0, order[None, :], 2 * N_CTX - 1 - order[None, :])
    tiles = doc_ids.reshape(SEQS, 2 * N_CTX, HALF_STRETCH)
    laid = tiles[:, placed.reshape(-1)].reshape(SEQS, 2, N_CTX, HALF_STRETCH)
    return (order, laid.astype(jnp.int32))


def draw_stretch_order(key, part):
    return layout_tables(key)[0]


def draw_segments(key, part):
    return layout_tables(key)[1]


def level_of(stream_key, extent, cuts, smallest, high):
    def one(axis_at, shards_of):
        heights = jax.random.uniform(jax.random.fold_in(jax.random.fold_in(stream_key, 6), axis_at), (shards_of,), jnp.float32, smallest / len(cuts), high / len(cuts))
        return jnp.repeat(jnp.exp(heights), extent[axis_at] // shards_of).reshape((-1,) + (1,) * (len(extent) - axis_at - 1))

    loudness = one(*cuts[0])
    for cut in cuts[1:]:
        loudness = loudness * one(*cut)
    return loudness


def centred(stream_key, dims, deviation, reach, cuts=(), held_as=jnp.bfloat16):
    gain = level_of(stream_key, dims, cuts, -0.22, 0.18) if cuts else 1.0
    values = jax.random.normal(stream_key, dims, jnp.float32) * deviation * gain
    return jnp.minimum(jnp.maximum(values, -reach), reach).astype(held_as)


def setup_inputs(seed: int = 0) -> dict:
    streams_of = jax.random.split(jax.random.key(seed), 11)
    tokens = centred(streams_of[0], (SEQS, 2, N_CTX, HALF_STRETCH, D), 1.0, 6.0, ((2, 4), (3, 4)))
    segments = draw_segments(jax.random.fold_in(streams_of[10], 71), 0)
    stretch_order = draw_stretch_order(jax.random.fold_in(streams_of[10], 71), 0)
    norm_gains = jnp.clip(1.0 + 0.15 * jax.random.normal(streams_of[3], (4, D), jnp.float32), 0.25, 1.75)
    query_proj = centred(streams_of[4], (D, HEADS * HEAD_DIM), D ** -0.5, 0.125, ((0, 4), (1, 2)))
    keyval_proj = centred(streams_of[5], (D, 2, KV_HEADS * HEAD_DIM), D ** -0.5, 0.125, ((0, 4), (2, 2)))
    attn_proj = centred(streams_of[6], (D, HEADS * HEAD_DIM), (HEADS * HEAD_DIM) ** -0.5, 0.125, ((0, 4), (1, 2)))
    ffn_in = centred(streams_of[7], (D, 2, FF), D ** -0.5, 0.125, ((0, 4), (2, 2)))
    ffn_out = centred(streams_of[8], (D, FF), FF ** -0.5, 0.0625, ((0, 4), (1, 2)))
    cotangent = centred(streams_of[9], (SEQS, 2, N_CTX, HALF_STRETCH, D), 1.0, 6.0, ((2, 4), (3, 4)))
    return {"tokens": tokens, "segments": segments, "stretch_order": stretch_order, "norm_gains": norm_gains, "query_proj": query_proj, "keyval_proj": keyval_proj, "attn_proj": attn_proj, "ffn_in": ffn_in, "ffn_out": ffn_out, "cotangent": cotangent}


SOFT_CAP = 50.0
NORM_EPS = 1e-06

def rms_factor(values):
    return lax.rsqrt(lax.optimization_barrier(jnp.mean(values * values, axis=-1, keepdims=True)) + NORM_EPS)

def norm_back(grad_out, values, scale_gain):
    factor = rms_factor(values)
    normed = values * factor
    grad_gain = lax.optimization_barrier(jnp.sum(grad_out * normed, axis=0))
    scaled_grad = grad_out * scale_gain
    grad_in = factor * (scaled_grad - normed * lax.optimization_barrier(jnp.mean(scaled_grad * normed, axis=-1, keepdims=True)))
    return (grad_in, grad_gain)

def gelu_parts(gate_vals):
    values, pullback = jax.vjp(lambda inputs: jax.nn.gelu(inputs, approximate=True), gate_vals)
    return (values, pullback(jnp.ones_like(gate_vals))[0])

def round_trip(values):
    return lax.optimization_barrier(values.astype(jnp.bfloat16)).astype(jnp.float32)

def token_positions(stretch_order):
    ctx_count = stretch_order.shape[0]
    shape_all = (2, ctx_count, HALF_STRETCH)
    halves = lax.broadcasted_iota(jnp.int32, shape_all, 0)
    within = lax.broadcasted_iota(jnp.int32, shape_all, 2)
    paired = jnp.broadcast_to(stretch_order[None, :, None], shape_all)
    placed = jnp.where(halves == 0, paired, 2 * ctx_count - 1 - paired)
    return (placed * HALF_STRETCH + within).reshape(-1).astype(jnp.int32)

def capped_scores(query_blk, keys, query_pos, query_seg, key_pos, key_seg):
    raw_scores = jnp.einsum('qkge,bke->kgqb', query_blk.astype(jnp.float32), keys.astype(jnp.float32)) * HEAD_DIM ** (-0.5)
    capped = SOFT_CAP * jnp.tanh(raw_scores / SOFT_CAP)
    allowed = (query_seg[:, None] == key_seg[None, :]) & (key_pos[None, :] <= query_pos[:, None])
    return (capped, allowed[None, None])

def reference(tokens, segments, stretch_order, norm_gains, query_proj, keyval_proj, attn_proj, ffn_in, ffn_out, cotangent):
    row_count = SEQS * LENGTH
    qcols = HEADS * HEAD_DIM
    kcols = KV_HEADS * HEAD_DIM
    group = HEADS // KV_HEADS
    query_block = math.gcd(LENGTH, 512)
    block_count = LENGTH // query_block
    ffn_block = math.gcd(row_count, 4096)
    f32 = jnp.float32
    bf16 = jnp.bfloat16
    gain_pre, gain_post, gain_ffn, gain_last = (norm_gains[0], norm_gains[1], norm_gains[2], norm_gains[3])
    tok_in = tokens.reshape(row_count, D).astype(f32)
    xnorm = (tok_in * rms_factor(tok_in) * gain_pre).astype(bf16)
    query = jnp.dot(xnorm, query_proj, preferred_element_type=f32).astype(bf16)
    keyval = jnp.dot(xnorm, keyval_proj.reshape(D, 2 * kcols), preferred_element_type=f32).astype(bf16)
    positions = token_positions(stretch_order)
    seg_all = segments.reshape(SEQS, LENGTH)
    query_five = query.reshape(SEQS, LENGTH, KV_HEADS, group, HEAD_DIM)
    keyval_five = keyval.reshape(SEQS, LENGTH, 2, KV_HEADS, HEAD_DIM)

    def forward_seq(seq_index):
        seq_query = query_five[seq_index]
        seq_keys = keyval_five[seq_index, :, 0]
        seq_vals = keyval_five[seq_index, :, 1]
        seq_segs = seg_all[seq_index]

        def forward_block(block_index):
            first = block_index * query_block
            query_blk = lax.dynamic_slice_in_dim(seq_query, first, query_block, 0)
            query_pos = lax.dynamic_slice_in_dim(positions, first, query_block, 0)
            query_seg = lax.dynamic_slice_in_dim(seq_segs, first, query_block, 0)
            capped, allowed = capped_scores(query_blk, seq_keys, query_pos, query_seg, positions, seq_segs)
            expo = jnp.where(allowed, jnp.exp(capped), 0.0)
            denom = lax.optimization_barrier(jnp.sum(expo, axis=-1))
            mixture = jnp.einsum('kgqb,bke->qkge', round_trip(expo), seq_vals.astype(f32))
            attended_blk = (mixture / jnp.transpose(denom, (2, 0, 1))[..., None]).astype(bf16)
            return (attended_blk, jnp.log(denom))
        return lax.map(forward_block, jnp.arange(block_count, dtype=jnp.int32))
    attended_all, lse_all = lax.map(forward_seq, jnp.arange(SEQS, dtype=jnp.int32))
    attended = attended_all.reshape(row_count, qcols)
    branch = jnp.dot(attended, attn_proj.T, preferred_element_type=f32)
    hidden = tok_in + branch * rms_factor(branch) * gain_post
    cot_all = cotangent.reshape(row_count, D).astype(f32)
    in_flat = ffn_in.reshape(D, 2 * FF)

    def ffn_step(running, blocks):
        acc_in, acc_out, acc_ffn, acc_last = running
        hid_blk, cot_blk = blocks
        hnorm = (hid_blk * rms_factor(hid_blk) * gain_ffn).astype(bf16)
        both = jnp.dot(hnorm, in_flat, preferred_element_type=f32).reshape(-1, 2, FF)
        gelu_vals, gelu_slope = gelu_parts(both[:, 0])
        middle = (gelu_vals * both[:, 1]).astype(bf16)
        ffout = jnp.dot(middle, ffn_out.T, preferred_element_type=f32)
        out_blk = (hid_blk + ffout * rms_factor(ffout) * gain_last).astype(bf16)
        grad_ff, grad_last = norm_back(cot_blk, ffout, gain_last)
        grad_ffb = grad_ff.astype(bf16)
        grad_mid = jnp.dot(grad_ffb, ffn_out, preferred_element_type=f32)
        grad_both = jnp.stack([grad_mid * both[:, 1] * gelu_slope, grad_mid * gelu_vals], axis=1).astype(bf16).reshape(-1, 2 * FF)
        grad_hn = jnp.dot(grad_both, in_flat.T, preferred_element_type=f32)
        grad_hid_n, grad_ffn = norm_back(grad_hn, hid_blk, gain_ffn)
        grad_hid = cot_blk + grad_hid_n
        acc_in = acc_in + jnp.dot(hnorm.T, grad_both, preferred_element_type=f32)
        acc_out = acc_out + jnp.dot(grad_ffb.T, middle, preferred_element_type=f32)
        return ((acc_in, acc_out, acc_ffn + grad_ffn, acc_last + grad_last), (out_blk, grad_hid))
    start_acc = (jnp.zeros((D, 2 * FF), f32), jnp.zeros((D, FF), f32), jnp.zeros((D,), f32), jnp.zeros((D,), f32))
    ffn_sums, ffn_rows = lax.scan(ffn_step, start_acc, (hidden.reshape(-1, ffn_block, D), cot_all.reshape(-1, ffn_block, D)))
    grad_in_w, grad_out_w, grad_ffn_gain, grad_last_gain = ffn_sums
    result = ffn_rows[0].reshape(tokens.shape)
    grad_hidden = ffn_rows[1].reshape(row_count, D)
    grad_branch, grad_post_gain = norm_back(grad_hidden, branch, gain_post)
    grad_branchb = grad_branch.astype(bf16)
    grad_attended = jnp.dot(grad_branchb, attn_proj, preferred_element_type=f32).astype(bf16)
    grad_attn = jnp.dot(grad_branchb.T, attended, preferred_element_type=f32)
    grad_att_five = grad_attended.reshape(SEQS, LENGTH, KV_HEADS, group, HEAD_DIM)
    att_five = attended.reshape(SEQS, LENGTH, KV_HEADS, group, HEAD_DIM)

    def backward_seq(seq_index):
        seq_query = query_five[seq_index]
        seq_keys = keyval_five[seq_index, :, 0]
        seq_vals = keyval_five[seq_index, :, 1]
        seq_segs = seg_all[seq_index]
        seq_grad = grad_att_five[seq_index]
        seq_att = att_five[seq_index]
        seq_lse = lse_all[seq_index]

        def backward_block(running, block_index):
            grad_keys, grad_vals = running
            first = block_index * query_block
            query_blk = lax.dynamic_slice_in_dim(seq_query, first, query_block, 0)
            grad_blk = lax.dynamic_slice_in_dim(seq_grad, first, query_block, 0).astype(f32)
            att_blk = lax.dynamic_slice_in_dim(seq_att, first, query_block, 0).astype(f32)
            query_pos = lax.dynamic_slice_in_dim(positions, first, query_block, 0)
            query_seg = lax.dynamic_slice_in_dim(seq_segs, first, query_block, 0)
            lse_blk = lax.dynamic_index_in_dim(seq_lse, block_index, 0, keepdims=False)
            capped, allowed = capped_scores(query_blk, seq_keys, query_pos, query_seg, positions, seq_segs)
            prob = jnp.where(allowed, jnp.exp(capped - lse_blk[..., None]), 0.0)
            delta = jnp.einsum('qkge,qkge->kgq', grad_blk, att_blk)
            grad_prob = jnp.einsum('qkge,bke->kgqb', grad_blk, seq_vals.astype(f32))
            ratio = capped / SOFT_CAP
            grad_raw = prob * (grad_prob - delta[..., None]) * (1.0 - ratio * ratio) * HEAD_DIM ** (-0.5)
            raw_round = round_trip(grad_raw)
            prob_round = round_trip(prob)
            grad_query_blk = jnp.einsum('kgqb,bke->qkge', raw_round, seq_keys.astype(f32)).astype(bf16)
            grad_keys = grad_keys + jnp.einsum('kgqb,qkge->bke', raw_round, query_blk.astype(f32))
            grad_vals = grad_vals + jnp.einsum('kgqb,qkge->bke', prob_round, grad_blk)
            return ((grad_keys, grad_vals), grad_query_blk)
        zero_kv = jnp.zeros((LENGTH, KV_HEADS, HEAD_DIM), f32)
        sums_kv, grad_queries = lax.scan(backward_block, (zero_kv, zero_kv), jnp.arange(block_count, dtype=jnp.int32))
        return (grad_queries, jnp.stack([sums_kv[0], sums_kv[1]], axis=1).astype(bf16))
    grad_query_all, grad_keyval_all = lax.map(backward_seq, jnp.arange(SEQS, dtype=jnp.int32))
    grad_q_rows = grad_query_all.reshape(row_count, qcols)
    grad_kv_rows = grad_keyval_all.reshape(row_count, 2 * kcols)
    grad_xnorm = jnp.dot(grad_q_rows, query_proj.T, preferred_element_type=f32) + jnp.dot(grad_kv_rows, keyval_proj.reshape(D, 2 * kcols).T, preferred_element_type=f32)
    grad_x_n, grad_pre_gain = norm_back(grad_xnorm, tok_in, gain_pre)
    grad_tokens = (grad_hidden + grad_x_n).reshape(tokens.shape)
    grad_gains = jnp.stack([grad_pre_gain, grad_post_gain, grad_ffn_gain, grad_last_gain], axis=0)
    grad_query = jnp.dot(xnorm.T, grad_q_rows, preferred_element_type=f32)
    grad_keyval = jnp.dot(xnorm.T, grad_kv_rows, preferred_element_type=f32).reshape(D, 2, kcols)
    return (result, grad_tokens, grad_gains, grad_query, grad_keyval, grad_attn, grad_in_w.reshape(D, 2, FF), grad_out_w)
```

```python
import jax
import jax.numpy as jnp
from jax import lax
from jax.sharding import PartitionSpec as P

HEAD_DIM = 256
SOFT_CAP = 50.0
NORM_EPS = 1e-06

F32 = jnp.float32
BF16 = jnp.bfloat16


def rms_factor(values):
    return lax.rsqrt(jnp.mean(values * values, axis=-1, keepdims=True) + NORM_EPS)


def norm_back(grad_out, values, scale_gain):
    factor = rms_factor(values)
    normed = values * factor
    grad_gain = jnp.sum(grad_out * normed, axis=0)
    scaled_grad = grad_out * scale_gain
    grad_in = factor * (
        scaled_grad - normed * jnp.mean(scaled_grad * normed, axis=-1, keepdims=True)
    )
    return (grad_in, grad_gain)


def gelu_parts(gate_vals):
    values, pullback = jax.vjp(lambda inputs: jax.nn.gelu(inputs, approximate=True), gate_vals)
    return (values, pullback(jnp.ones_like(gate_vals))[0])


def dot_nn(left, right):
    return jnp.dot(left, right, preferred_element_type=F32)


def dot_nt(left, right):
    return lax.dot_general(left, right, (((1,), (1,)), ((), ())), preferred_element_type=F32)


def dot_tn(left, right):
    return lax.dot_general(left, right, (((0,), (0,)), ((), ())), preferred_element_type=F32)


def swap(values, axis_name, offset):
    count = lax.axis_size(axis_name)
    return lax.ppermute(values, axis_name, [(i, i ^ offset) for i in range(count)])


def gather_xor(values, axis_name):
    count = lax.axis_size(axis_name)
    return jnp.stack([values] + [swap(values, axis_name, j) for j in range(1, count)])


def scatter_xor(parts, axis_name):
    total = parts[0].astype(F32)
    for j in range(1, lax.axis_size(axis_name)):
        total = total + swap(parts[j].astype(BF16), axis_name, j).astype(F32)
    return total


def gather_rows(rows):
    near = gather_xor(rows, "ctx").reshape(-1, rows.shape[-1])
    return gather_xor(near, "tp").reshape(-1, rows.shape[-1])


def scatter_rows(partial):
    width = partial.shape[-1]
    near = scatter_xor(partial.reshape(lax.axis_size("tp"), -1, width), "tp")
    return scatter_xor(near.reshape(lax.axis_size("ctx"), -1, width), "ctx")


def sum_all(values):
    for axis_name in ("tp", "ctx", "fsdp"):
        offset = 1
        while offset < lax.axis_size(axis_name):
            values = values + swap(values, axis_name, offset)
            offset *= 2
    return values


def xor_order(values, own_at, axis):
    offset = 1
    while offset < values.shape[axis]:
        halves = values.reshape(values.shape[:axis] + (-1, 2, offset) + values.shape[axis + 1 :])
        turned = jnp.flip(halves, axis + 1)
        if isinstance(own_at, int):
            picked = turned if own_at & offset else halves
        else:
            picked = jnp.where((own_at & offset) != 0, turned, halves)
        values = picked.reshape(values.shape)
        offset *= 2
    return values


def cols(values, start, width):
    return lax.dynamic_slice_in_dim(values, start, width, axis=values.ndim - 1)


def on_device(
    tokens,
    segments,
    stretch_order,
    norm_gains,
    query_proj,
    keyval_proj,
    attn_proj,
    ffn_in,
    ffn_out,
    cotangent,
):
    seq_count, _, _, half_dev, width = tokens.shape
    fsdp_count = lax.axis_size("fsdp")
    ctx_count = lax.axis_size("ctx")
    tp_count = lax.axis_size("tp")
    fsdp_at, ctx_at, tp_at = (lax.axis_index(name) for name in ("fsdp", "ctx", "tp"))
    row_count = seq_count * 2 * half_dev
    own_count = row_count // tp_count
    group_rows = own_count * tp_count * ctx_count
    assert seq_count == tp_count

    head_count = query_proj.shape[1] // HEAD_DIM
    group = head_count // (keyval_proj.shape[2] // HEAD_DIM)
    repeat = ctx_count // head_count
    assert repeat >= 1 and repeat * head_count == ctx_count
    sharers = group * repeat
    head_at = ctx_at // repeat
    kv_at = ctx_at // sharers
    share_at = ctx_at % sharers
    q_width = HEAD_DIM // repeat
    kv_width = 2 * HEAD_DIM // sharers
    q_own = (ctx_at % repeat) * q_width
    kv_own = share_at * kv_width
    ff_width = ffn_out.shape[1] // ctx_count
    ff_at = ctx_at * ff_width

    qkv_part = jnp.concatenate(
        [
            cols(query_proj, head_at * HEAD_DIM, HEAD_DIM),
            cols(keyval_proj[:, 0], kv_at * HEAD_DIM, HEAD_DIM),
            cols(keyval_proj[:, 1], kv_at * HEAD_DIM, HEAD_DIM),
        ],
        axis=1,
    )
    attn_part = cols(attn_proj, head_at * HEAD_DIM, HEAD_DIM)
    in_part = jnp.concatenate(
        [cols(ffn_in[:, 0], ff_at, ff_width), cols(ffn_in[:, 1], ff_at, ff_width)], axis=1
    )
    out_part = cols(ffn_out, ff_at, ff_width)
    w_qkv, w_attn, w_in, w_out = (
        lax.all_gather(part, "fsdp", axis=0, tiled=True)
        for part in (qkv_part, attn_part, in_part, out_part)
    )

    gain_pre, gain_post, gain_ffn, gain_last = (norm_gains[i] for i in range(4))
    row_at = tp_at * own_count
    tok_in = lax.dynamic_slice_in_dim(
        tokens.reshape(row_count, width), row_at, own_count, 0
    ).astype(F32)
    cot_in = lax.dynamic_slice_in_dim(
        cotangent.reshape(row_count, width), row_at, own_count, 0
    ).astype(F32)

    half_stretch = half_dev * fsdp_count
    seg_all = lax.all_gather(
        segments.reshape(seq_count, 2, half_dev), ("fsdp", "ctx"), axis=0, tiled=False
    ).reshape(fsdp_count, ctx_count, seq_count, 2, half_dev)
    ctx_ids = ctx_at ^ jnp.arange(ctx_count)
    fsdp_ids = fsdp_at ^ jnp.arange(fsdp_count)
    key_seg = xor_order(xor_order(xor_order(seg_all, fsdp_at, 0), ctx_at, 1), tp_at, 2)
    key_seg = key_seg.transpose(2, 0, 1, 3, 4)
    query_seg = key_seg[:, 0].reshape(seq_count, -1)
    key_seg = key_seg.reshape(seq_count, -1)
    paired = xor_order(stretch_order, ctx_at, 0)
    blocks = jnp.stack([paired, 2 * ctx_count - 1 - paired], axis=1)
    key_pos = (
        blocks[None, :, :, None] * half_stretch
        + fsdp_ids[:, None, None, None] * half_dev
        + jnp.arange(half_dev)[None, None, None, :]
    )
    query_pos = key_pos[0].reshape(-1)
    key_pos = key_pos.reshape(-1)
    allowed = (query_seg[:, :, None] == key_seg[:, None, :]) & (
        key_pos[None, None, :] <= query_pos[None, :, None]
    )

    xnorm_own = (tok_in * rms_factor(tok_in) * gain_pre).astype(BF16)
    xnorm = gather_rows(xnorm_own)
    qkv = dot_nn(xnorm, w_qkv).astype(BF16)
    query = qkv[:, :HEAD_DIM].reshape(seq_count, -1, HEAD_DIM)
    kv_own_rows = qkv[:, HEAD_DIM:].reshape(seq_count, -1, 2 * HEAD_DIM)
    kv_all = jnp.concatenate(
        [kv_own_rows] + [swap(kv_own_rows, "fsdp", j) for j in range(1, fsdp_count)], axis=1
    )
    keys, vals = kv_all[:, :, :HEAD_DIM], kv_all[:, :, HEAD_DIM:]
    raw_scores = jnp.einsum("sqe,ske->sqk", query, keys, preferred_element_type=F32)
    capped = SOFT_CAP * jnp.tanh(raw_scores * (HEAD_DIM ** (-0.5) / SOFT_CAP))
    expo = jnp.where(allowed, jnp.exp(capped), 0.0)
    denom = jnp.sum(expo, axis=-1, keepdims=True)
    mixture = jnp.einsum("sqk,ske->sqe", expo.astype(BF16), vals, preferred_element_type=F32)
    attended_seq = (mixture / denom).astype(BF16)
    lse = jnp.log(denom)
    attended = attended_seq.reshape(group_rows, HEAD_DIM)
    attended_own = attended if repeat == 1 else cols(attended, q_own, q_width)
    w_attn_own = w_attn if repeat == 1 else cols(w_attn, q_own, q_width)
    branch = scatter_rows(dot_nt(attended_own, w_attn_own))

    hidden = tok_in + branch * rms_factor(branch) * gain_post
    hnorm = gather_rows((hidden * rms_factor(hidden) * gain_ffn).astype(BF16))
    both = dot_nn(hnorm, w_in)
    gate, up = both[:, :ff_width], both[:, ff_width:]
    gelu_vals, gelu_slope = gelu_parts(gate)
    middle = (gelu_vals * up).astype(BF16)
    ffout = scatter_rows(dot_nt(middle, w_out))
    result = (hidden + ffout * rms_factor(ffout) * gain_last).astype(BF16)

    grad_ff, grad_last_gain = norm_back(cot_in, ffout, gain_last)
    grad_ffb = gather_rows(grad_ff.astype(BF16))
    grad_mid = dot_nn(grad_ffb, w_out)
    grad_both = jnp.concatenate(
        [grad_mid * up * gelu_slope, grad_mid * gelu_vals], axis=1
    ).astype(BF16)

    def weight_grad(left, right):
        return lax.psum_scatter(
            dot_tn(left, right).astype(BF16), "fsdp", scatter_dimension=0, tiled=True
        )

    def spread(part):
        return lax.all_gather(part, "ctx", axis=0, tiled=False)

    all_out = spread(weight_grad(grad_ffb, middle))
    all_in = spread(weight_grad(hnorm, grad_both))

    grad_hn = scatter_rows(dot_nt(grad_both, w_in))
    grad_hid_n, grad_ffn_gain = norm_back(grad_hn, hidden, gain_ffn)
    grad_hidden = cot_in + grad_hid_n
    grad_branch, grad_post_gain = norm_back(grad_hidden, branch, gain_post)
    grad_branchb = gather_rows(grad_branch.astype(BF16))

    grad_attended = dot_nn(grad_branchb, w_attn).astype(BF16)
    grad_att_seq = grad_attended.reshape(seq_count, -1, HEAD_DIM)
    delta = jnp.sum(
        grad_att_seq.astype(F32) * attended_seq.astype(F32), axis=-1, keepdims=True
    )
    prob = jnp.where(allowed, jnp.exp(capped - lse), 0.0)
    grad_prob = jnp.einsum("sqe,ske->sqk", grad_att_seq, vals, preferred_element_type=F32)
    ratio = capped / SOFT_CAP
    grad_raw = prob * (grad_prob - delta) * (1.0 - ratio * ratio) * HEAD_DIM ** (-0.5)
    raw_half = grad_raw.astype(BF16)
    prob_half = prob.astype(BF16)
    grad_q = jnp.einsum("sqk,ske->sqe", raw_half, keys, preferred_element_type=F32).astype(BF16)
    grad_k = jnp.einsum("sqk,sqe->ske", raw_half, query, preferred_element_type=F32)
    grad_v = jnp.einsum("sqk,sqe->ske", prob_half, grad_att_seq, preferred_element_type=F32)
    pieces = jnp.stack([grad_k, grad_v])
    pieces = pieces.reshape(2, *grad_k.shape[:2], sharers // 2, kv_width)
    pieces = pieces.transpose(0, 3, 1, 2, 4).reshape(sharers, *grad_k.shape[:2], kv_width)
    kv_term = lax.dynamic_index_in_dim(pieces, share_at, 0, keepdims=False)
    for j in range(repeat, sharers, repeat):
        sent = lax.dynamic_index_in_dim(pieces, share_at ^ j, 0, keepdims=False).astype(BF16)
        by_ctx = sent.reshape(seq_count, fsdp_count, ctx_count, -1, kv_width)
        sent = xor_order(by_ctx, j, 2).reshape(sent.shape)
        kv_term = kv_term + swap(sent, "ctx", j).astype(F32)
    kv_term = kv_term.reshape(seq_count, fsdp_count, -1, kv_width).transpose(1, 0, 2, 3)
    grad_kv = scatter_xor(kv_term, "fsdp").astype(BF16).reshape(group_rows, kv_width)
    grad_q = grad_q.reshape(group_rows, HEAD_DIM)
    grad_q_own = grad_q if repeat == 1 else cols(grad_q, q_own, q_width)
    grad_qkv = jnp.concatenate([grad_q_own, grad_kv], axis=1)
    w_q_own = w_qkv[:, :HEAD_DIM] if repeat == 1 else cols(w_qkv, q_own, q_width)
    w_qkv_own = jnp.concatenate([w_q_own, cols(w_qkv, HEAD_DIM + kv_own, kv_width)], axis=1)
    grad_xnorm = scatter_rows(dot_nt(grad_qkv, w_qkv_own))
    grad_x_n, grad_pre_gain = norm_back(grad_xnorm, tok_in, gain_pre)
    grad_tokens_own = grad_hidden + grad_x_n

    all_attn = spread(weight_grad(grad_branchb, attended_own))
    all_qkv = spread(weight_grad(xnorm, grad_qkv))

    own_width = all_out.shape[1]
    grad_gains = sum_all(
        jnp.stack([grad_pre_gain, grad_post_gain, grad_ffn_gain, grad_last_gain], axis=0)
    )
    result = lax.all_gather(result, "tp", axis=0, tiled=True)
    grad_tokens = lax.all_gather(grad_tokens_own, "tp", axis=0, tiled=True)

    def columns(spread_grad):
        return jnp.moveaxis(spread_grad, 0, -2).astype(F32)

    grad_query = columns(all_qkv[:, :, :q_width]).reshape(own_width, -1)
    grad_keyval = (
        all_qkv[:, :, q_width:]
        .reshape(ctx_count // sharers, 2, sharers // 2, own_width, kv_width)
        .transpose(3, 1, 0, 2, 4)
        .astype(F32)
        .reshape(own_width, 2, -1)
    )
    grad_attn = columns(all_attn).reshape(own_width, -1)
    grad_ffn_in = columns(all_in.reshape(ctx_count, own_width, 2, ff_width)).reshape(
        own_width, 2, -1
    )
    grad_ffn_out = columns(all_out).reshape(own_width, -1)
    return (
        result.reshape(tokens.shape),
        grad_tokens.reshape(tokens.shape),
        grad_gains,
        grad_query,
        grad_keyval,
        grad_attn,
        grad_ffn_in,
        grad_ffn_out,
    )


def solution(mesh):
    placed = (
        P(None, None, "ctx", "fsdp", None),
        P(None, None, "ctx", "fsdp"),
        P(),
        P(),
        P("fsdp", "tp"),
        P("fsdp", None, "tp"),
        P("fsdp", "tp"),
        P("fsdp", None, "tp"),
        P("fsdp", "tp"),
        P(None, None, "ctx", "fsdp", None),
    )
    return jax.shard_map(
        on_device,
        mesh=mesh,
        in_specs=placed,
        out_specs=(
            P(None, None, "ctx", "fsdp", None),
            P(None, None, "ctx", "fsdp", None),
            P(),
            P("fsdp", "tp"),
            P("fsdp", None, "tp"),
            P("fsdp", "tp"),
            P("fsdp", None, "tp"),
            P("fsdp", "tp"),
        ),
        check_vma=False,
    )
```

```python
import jax
import jax.numpy as jnp
from jax import lax
from jax.sharding import PartitionSpec as P

HEAD_DIM = 256
SOFT_CAP = 50.0
NORM_EPS = 1e-06

F32 = jnp.float32
BF16 = jnp.bfloat16


def rms_factor(values):
    return lax.rsqrt(jnp.mean(values * values, axis=-1, keepdims=True) + NORM_EPS)


def norm_back(grad_out, values, scale_gain):
    factor = rms_factor(values)
    normed = values * factor
    grad_gain = jnp.sum(grad_out * normed, axis=0)
    scaled_grad = grad_out * scale_gain
    grad_in = factor * (
        scaled_grad - normed * jnp.mean(scaled_grad * normed, axis=-1, keepdims=True)
    )
    return (grad_in, grad_gain)


def gelu_parts(gate_vals):
    values, pullback = jax.vjp(lambda inputs: jax.nn.gelu(inputs, approximate=True), gate_vals)
    return (values, pullback(jnp.ones_like(gate_vals))[0])


def dot_nn(left, right):
    return jnp.dot(left, right, preferred_element_type=F32)


def dot_nt(left, right):
    return lax.dot_general(left, right, (((1,), (1,)), ((), ())), preferred_element_type=F32)


def dot_tn(left, right):
    return lax.dot_general(left, right, (((0,), (0,)), ((), ())), preferred_element_type=F32)


def swap(values, axis_name, offset):
    count = lax.axis_size(axis_name)
    return lax.ppermute(values, axis_name, [(i, i ^ offset) for i in range(count)])


def gather_xor(values, axis_name):
    count = lax.axis_size(axis_name)
    held = {0: values}
    offset = count // 2
    while offset:
        for j in tuple(held):
            held[j ^ offset] = swap(held[j], axis_name, offset)
        offset //= 2
    return [held[j] for j in range(count)]


def scatter_xor(parts, axis_name):
    count = lax.axis_size(axis_name)
    held = {j: parts[j] for j in range(count)}
    offset = 1
    while offset < count:
        sent = [j for j in range(offset, count) if j & offset and j % offset == 0]
        for j in reversed(sent):
            got = swap(held.pop(j).astype(BF16), axis_name, offset)
            held[j ^ offset] = held[j ^ offset].astype(F32) + got.astype(F32)
        offset *= 2
    return held[0]


def gather_rows(rows):
    near = jnp.concatenate(gather_xor(rows, "ctx"), axis=0)
    return jnp.concatenate(gather_xor(near, "tp"), axis=0)


def scatter_rows(partial):
    near = scatter_xor(jnp.split(partial, lax.axis_size("tp")), "tp")
    return scatter_xor(jnp.split(near, lax.axis_size("ctx")), "ctx")


def after(values, *others):
    return lax.optimization_barrier((values, *others))[0]


def both_cores(own, tp_at):
    other = swap(own, "tp", 1)
    first = jnp.where(tp_at == 0, own, other)
    second = jnp.where(tp_at == 0, other, own)
    return jnp.concatenate([first, second], axis=0)


def sum_all(values):
    for axis_name in ("tp", "ctx", "fsdp"):
        offset = 1
        while offset < lax.axis_size(axis_name):
            values = values + swap(values, axis_name, offset)
            offset *= 2
    return values


def xor_order(values, own_at, axis):
    offset = 1
    while offset < values.shape[axis]:
        halves = values.reshape(values.shape[:axis] + (-1, 2, offset) + values.shape[axis + 1 :])
        turned = jnp.flip(halves, axis + 1)
        if isinstance(own_at, int):
            picked = turned if own_at & offset else halves
        else:
            picked = jnp.where((own_at & offset) != 0, turned, halves)
        values = picked.reshape(values.shape)
        offset *= 2
    return values


def cols(values, start, width):
    return lax.dynamic_slice_in_dim(values, start, width, axis=values.ndim - 1)


def on_device(
    tokens,
    segments,
    stretch_order,
    norm_gains,
    query_proj,
    keyval_proj,
    attn_proj,
    ffn_in,
    ffn_out,
    cotangent,
):
    seq_count, _, _, half_dev, width = tokens.shape
    fsdp_count = lax.axis_size("fsdp")
    ctx_count = lax.axis_size("ctx")
    tp_count = lax.axis_size("tp")
    fsdp_at, ctx_at, tp_at = (lax.axis_index(name) for name in ("fsdp", "ctx", "tp"))
    row_count = seq_count * 2 * half_dev
    own_count = row_count // tp_count
    group_rows = own_count * tp_count * ctx_count
    assert seq_count == tp_count

    head_count = query_proj.shape[1] // HEAD_DIM
    group = head_count // (keyval_proj.shape[2] // HEAD_DIM)
    repeat = ctx_count // head_count
    assert repeat >= 1 and repeat * head_count == ctx_count
    sharers = group * repeat
    head_at = ctx_at // repeat
    kv_at = ctx_at // sharers
    share_at = ctx_at % sharers
    q_width = HEAD_DIM // repeat
    kv_width = 2 * HEAD_DIM // sharers
    q_own = (ctx_at % repeat) * q_width
    kv_own = share_at * kv_width
    ff_width = ffn_out.shape[1] // ctx_count
    ff_at = ctx_at * ff_width

    kv_part = cols(keyval_proj, kv_at * HEAD_DIM, HEAD_DIM)
    att_part = jnp.concatenate(
        [
            cols(query_proj, head_at * HEAD_DIM, HEAD_DIM),
            kv_part[:, 0],
            kv_part[:, 1],
            cols(attn_proj, head_at * HEAD_DIM, HEAD_DIM),
        ],
        axis=1,
    )
    w_att = lax.all_gather(att_part, "fsdp", axis=0, tiled=True)
    w_qkv, w_attn = w_att[:, : 3 * HEAD_DIM], w_att[:, 3 * HEAD_DIM :]
    in_part = cols(ffn_in, ff_at, ff_width)
    ffn_part = jnp.concatenate(
        [in_part[:, 0], in_part[:, 1], cols(ffn_out, ff_at, ff_width)], axis=1
    )
    w_ffn = lax.all_gather(ffn_part, "fsdp", axis=0, tiled=True)
    w_in, w_out = w_ffn[:, : 2 * ff_width], w_ffn[:, 2 * ff_width :]

    gain_pre, gain_post, gain_ffn, gain_last = (norm_gains[i] for i in range(4))
    row_at = tp_at * own_count
    tok_in = lax.dynamic_slice_in_dim(
        tokens.reshape(row_count, width), row_at, own_count, 0
    ).astype(F32)
    cot_in = lax.dynamic_slice_in_dim(
        cotangent.reshape(row_count, width), row_at, own_count, 0
    ).astype(F32)

    half_stretch = half_dev * fsdp_count
    length = 2 * ctx_count * half_stretch
    slot = jnp.arange(ctx_count) == ctx_at
    paired = jnp.sum(jnp.where(slot, stretch_order, 0))
    block = jnp.stack([paired, 2 * ctx_count - 1 - paired])
    position = block[:, None] * half_stretch + fsdp_at * half_dev + jnp.arange(half_dev)
    marks = segments.reshape(seq_count, 2, half_dev) * length + position[None]
    marks = marks.reshape(seq_count, 1, 2 * half_dev)
    marks = jnp.concatenate(gather_xor(marks, "ctx"), axis=1).reshape(seq_count, 1, -1)
    marks = jnp.concatenate(gather_xor(marks, "fsdp"), axis=1)
    marks = jnp.where(tp_at == 0, marks, jnp.flip(marks, 0))
    query_mark = marks[:, 0]
    key_mark = marks.reshape(seq_count, -1)
    query_first = query_mark - lax.rem(query_mark, length)
    allowed = (key_mark[:, None, :] <= query_mark[:, :, None]) & (
        key_mark[:, None, :] >= query_first[:, :, None]
    )

    xnorm_own = (tok_in * rms_factor(tok_in) * gain_pre).astype(BF16)
    xnorm = gather_rows(xnorm_own)
    qkv = dot_nn(xnorm, w_qkv).astype(BF16)
    query = qkv[:, :HEAD_DIM].reshape(seq_count, -1, HEAD_DIM)
    kv_own_rows = qkv[:, HEAD_DIM:].reshape(seq_count, -1, 2 * HEAD_DIM)
    kv_all = jnp.concatenate(gather_xor(kv_own_rows, "fsdp"), axis=1)
    keys, vals = kv_all[:, :, :HEAD_DIM], kv_all[:, :, HEAD_DIM:]
    raw_scores = jnp.einsum("sqe,ske->sqk", query, keys, preferred_element_type=F32)
    capped = SOFT_CAP * jnp.tanh(raw_scores * (HEAD_DIM ** (-0.5) / SOFT_CAP))
    expo = jnp.where(allowed, jnp.exp(capped), 0.0)
    denom = jnp.sum(expo, axis=-1, keepdims=True)
    mixture = jnp.einsum("sqk,ske->sqe", expo.astype(BF16), vals, preferred_element_type=F32)
    attended_seq = (mixture / denom).astype(BF16)
    lse = jnp.log(denom)
    attended = attended_seq.reshape(group_rows, HEAD_DIM)
    attended_own = attended if repeat == 1 else cols(attended, q_own, q_width)
    w_attn_own = w_attn if repeat == 1 else cols(w_attn, q_own, q_width)
    branch = scatter_rows(dot_nt(attended_own, w_attn_own))

    hidden = tok_in + branch * rms_factor(branch) * gain_post
    hnorm = gather_rows((hidden * rms_factor(hidden) * gain_ffn).astype(BF16))
    both = dot_nn(hnorm, w_in)
    gate, up = both[:, :ff_width], both[:, ff_width:]
    gelu_vals, gelu_slope = gelu_parts(gate)
    middle = (gelu_vals * up).astype(BF16)
    ffout = scatter_rows(dot_nt(middle, w_out))
    result = (hidden + ffout * rms_factor(ffout) * gain_last).astype(BF16)

    grad_ff, grad_last_gain = norm_back(cot_in, ffout, gain_last)
    grad_ffb = gather_rows(grad_ff.astype(BF16))
    grad_mid = dot_nn(grad_ffb, w_out)
    grad_both = jnp.concatenate(
        [grad_mid * up * gelu_slope, grad_mid * gelu_vals], axis=1
    ).astype(BF16)

    def weight_grad(left, right):
        return lax.psum_scatter(
            dot_tn(left, right).astype(BF16), "fsdp", scatter_dimension=0, tiled=True
        )

    def spread(part):
        return lax.all_gather(part, "ctx", axis=0, tiled=False)

    part_out = weight_grad(grad_ffb, middle)
    part_in = weight_grad(hnorm, grad_both)

    grad_hn = scatter_rows(dot_nt(grad_both, w_in))
    grad_hid_n, grad_ffn_gain = norm_back(grad_hn, hidden, gain_ffn)
    grad_hidden = cot_in + grad_hid_n
    grad_branch, grad_post_gain = norm_back(grad_hidden, branch, gain_post)
    grad_branchb = gather_rows(grad_branch.astype(BF16))
    grad_branchb = after(grad_branchb, part_out)
    all_out = spread(part_out)

    grad_attended = dot_nn(grad_branchb, w_attn).astype(BF16)
    grad_att_seq = grad_attended.reshape(seq_count, -1, HEAD_DIM)
    delta = jnp.sum(
        grad_att_seq.astype(F32) * attended_seq.astype(F32), axis=-1, keepdims=True
    )
    prob = jnp.where(allowed, jnp.exp(capped - lse), 0.0)
    grad_prob = jnp.einsum("sqe,ske->sqk", grad_att_seq, vals, preferred_element_type=F32)
    ratio = capped / SOFT_CAP
    grad_raw = prob * (grad_prob - delta) * (1.0 - ratio * ratio) * HEAD_DIM ** (-0.5)
    raw_half = grad_raw.astype(BF16)
    prob_half = prob.astype(BF16)
    grad_q = jnp.einsum("sqk,ske->sqe", raw_half, keys, preferred_element_type=F32).astype(BF16)
    grad_k = jnp.einsum("sqk,sqe->ske", raw_half, query, preferred_element_type=F32)
    grad_v = jnp.einsum("sqk,sqe->ske", prob_half, grad_att_seq, preferred_element_type=F32)
    pieces = jnp.stack([grad_k, grad_v])
    pieces = pieces.reshape(2, *grad_k.shape[:2], sharers // 2, kv_width)
    pieces = pieces.transpose(0, 3, 1, 2, 4).reshape(sharers, *grad_k.shape[:2], kv_width)
    kv_term = lax.dynamic_index_in_dim(pieces, share_at, 0, keepdims=False)
    for j in range(repeat, sharers, repeat):
        sent = lax.dynamic_index_in_dim(pieces, share_at ^ j, 0, keepdims=False).astype(BF16)
        by_ctx = sent.reshape(seq_count, fsdp_count, ctx_count, -1, kv_width)
        sent = xor_order(by_ctx, j, 2).reshape(sent.shape)
        kv_term = kv_term + swap(sent, "ctx", j).astype(F32)
    kv_term = kv_term.reshape(seq_count, fsdp_count, -1, kv_width)
    grad_kv = scatter_xor([kv_term[:, j] for j in range(fsdp_count)], "fsdp").astype(BF16).reshape(group_rows, kv_width)
    grad_q = grad_q.reshape(group_rows, HEAD_DIM)
    grad_q_own = grad_q if repeat == 1 else cols(grad_q, q_own, q_width)
    grad_qkv = jnp.concatenate([grad_q_own, grad_kv], axis=1)
    grad_qkv = after(grad_qkv, part_in)
    own_width = part_in.shape[0]
    part_in = jnp.stack([part_in[:, :ff_width], part_in[:, ff_width:]], axis=1)
    all_in = spread(part_in)
    w_q_own = w_qkv[:, :HEAD_DIM] if repeat == 1 else cols(w_qkv, q_own, q_width)
    w_qkv_own = jnp.concatenate([w_q_own, cols(w_qkv, HEAD_DIM + kv_own, kv_width)], axis=1)
    grad_xnorm = scatter_rows(dot_nt(grad_qkv, w_qkv_own))
    grad_x_n, grad_pre_gain = norm_back(grad_xnorm, tok_in, gain_pre)
    grad_tokens_own = grad_hidden + grad_x_n

    att_term = jnp.concatenate(
        [dot_tn(xnorm, grad_qkv).astype(BF16), dot_tn(grad_branchb, attended_own).astype(BF16)],
        axis=1,
    )
    att_term = after(att_term, all_out)
    all_att = spread(lax.psum_scatter(att_term, "fsdp", scatter_dimension=0, tiled=True))
    all_qkv, all_attn = all_att[:, :, : q_width + kv_width], all_att[:, :, q_width + kv_width :]

    grad_gains = sum_all(
        jnp.stack([grad_pre_gain, grad_post_gain, grad_ffn_gain, grad_last_gain], axis=0)
    )
    result = both_cores(result, tp_at)
    grad_tokens = both_cores(grad_tokens_own, tp_at)

    def columns(spread_grad):
        return jnp.moveaxis(spread_grad, 0, -2).astype(F32)

    grad_query = columns(all_qkv[:, :, :q_width]).reshape(own_width, -1)
    grad_keyval = (
        all_qkv[:, :, q_width:]
        .reshape(ctx_count // sharers, 2, sharers // 2, own_width, kv_width)
        .transpose(3, 1, 0, 2, 4)
        .astype(F32)
        .reshape(own_width, 2, -1)
    )
    grad_attn = columns(all_attn).reshape(own_width, -1)
    grad_ffn_in = columns(all_in).reshape(own_width, 2, -1)
    grad_ffn_out = columns(all_out).reshape(own_width, -1)
    return (
        result.reshape(tokens.shape),
        grad_tokens.reshape(tokens.shape),
        grad_gains,
        grad_query,
        grad_keyval,
        grad_attn,
        grad_ffn_in,
        grad_ffn_out,
    )


def solution(mesh):
    placed = (
        P(None, None, "ctx", "fsdp", None),
        P(None, None, "ctx", "fsdp"),
        P(),
        P(),
        P("fsdp", "tp"),
        P("fsdp", None, "tp"),
        P("fsdp", "tp"),
        P("fsdp", None, "tp"),
        P("fsdp", "tp"),
        P(None, None, "ctx", "fsdp", None),
    )
    return jax.shard_map(
        on_device,
        mesh=mesh,
        in_specs=placed,
        out_specs=(
            P(None, None, "ctx", "fsdp", None),
            P(None, None, "ctx", "fsdp", None),
            P(),
            P("fsdp", "tp"),
            P("fsdp", None, "tp"),
            P("fsdp", "tp"),
            P("fsdp", None, "tp"),
            P("fsdp", "tp"),
        ),
        check_vma=False,
    )
```

```python
import jax
import jax.numpy as jnp
from jax import lax
from jax.experimental import pallas as pl
from jax.experimental.pallas import tpu as pltpu
from jax.sharding import PartitionSpec as P

HEAD_DIM = 256
SOFT_CAP = 50.0
NORM_EPS = 1e-06

F32 = jnp.float32
BF16 = jnp.bfloat16


def rms_factor(values):
    return lax.rsqrt(jnp.mean(values * values, axis=-1, keepdims=True) + NORM_EPS)


def norm_back(grad_out, values, scale_gain):
    factor = rms_factor(values)
    normed = values * factor
    grad_gain = jnp.sum(grad_out * normed, axis=0)
    scaled_grad = grad_out * scale_gain
    grad_in = factor * (
        scaled_grad - normed * jnp.mean(scaled_grad * normed, axis=-1, keepdims=True)
    )
    return (grad_in, grad_gain)


def gelu_parts(gate_vals):
    values, pullback = jax.vjp(lambda inputs: jax.nn.gelu(inputs, approximate=True), gate_vals)
    return (values, pullback(jnp.ones_like(gate_vals))[0])


def dot_nn(left, right):
    return jnp.dot(left, right, preferred_element_type=F32)


def dot_nt(left, right):
    return lax.dot_general(left, right, (((1,), (1,)), ((), ())), preferred_element_type=F32)


def dot_tn(left, right):
    return lax.dot_general(left, right, (((0,), (0,)), ((), ())), preferred_element_type=F32)


def swap(values, axis_name, offset):
    count = lax.axis_size(axis_name)
    return lax.ppermute(values, axis_name, [(i, i ^ offset) for i in range(count)])


def gather_xor(values, axis_name):
    count = lax.axis_size(axis_name)
    held = {0: values}
    offset = count // 2
    while offset:
        for j in tuple(held):
            held[j ^ offset] = swap(held[j], axis_name, offset)
        offset //= 2
    return [held[j] for j in range(count)]


def scatter_xor(parts, axis_name):
    count = lax.axis_size(axis_name)
    held = {j: parts[j] for j in range(count)}
    offset = 1
    while offset < count:
        sent = [j for j in range(offset, count) if j & offset and j % offset == 0]
        for j in reversed(sent):
            got = swap(held.pop(j).astype(BF16), axis_name, offset)
            held[j ^ offset] = held[j ^ offset].astype(F32) + got.astype(F32)
        offset *= 2
    return held[0]


def gather_weights(part, own_at):
    count = lax.axis_size("fsdp")
    hops = [1 << i for i in range(count.bit_length() - 1)]
    rows, width = part.shape
    half = width // 2
    whole = []
    for columns, order in ((part[:, :half], hops), (part[:, half:], hops[::-1])):
        held = {0: columns}
        for offset in order:
            for j in tuple(held):
                held[j ^ offset] = swap(held[j], "fsdp", offset)
        out = jnp.zeros((count * rows, columns.shape[1]), part.dtype)
        for j in range(count):
            out = lax.dynamic_update_slice_in_dim(out, held[j], (own_at ^ j) * rows, 0)
        whole.append(out)
    return whole


def gather_rows(rows):
    near = jnp.concatenate(gather_xor(rows, "ctx"), axis=0)
    return jnp.concatenate(gather_xor(near, "tp"), axis=0)


def scatter_rows(partial):
    near = scatter_xor(jnp.split(partial, lax.axis_size("tp")), "tp")
    return scatter_xor(jnp.split(near, lax.axis_size("ctx")), "ctx")


def after(values, *others):
    return lax.optimization_barrier((values, *others))[0]


def both_cores(own, tp_at):
    other = swap(own, "tp", 1)
    first = jnp.where(tp_at == 0, own, other)
    second = jnp.where(tp_at == 0, other, own)
    return jnp.concatenate([first, second], axis=0)


def sum_all(values):
    for axis_name in ("tp", "ctx", "fsdp"):
        offset = 1
        while offset < lax.axis_size(axis_name):
            values = values + swap(values, axis_name, offset)
            offset *= 2
    return values


def xor_order(values, own_at, axis):
    offset = 1
    while offset < values.shape[axis]:
        halves = values.reshape(values.shape[:axis] + (-1, 2, offset) + values.shape[axis + 1 :])
        turned = jnp.flip(halves, axis + 1)
        if isinstance(own_at, int):
            picked = turned if own_at & offset else halves
        else:
            picked = jnp.where((own_at & offset) != 0, turned, halves)
        values = picked.reshape(values.shape)
        offset *= 2
    return values


def spread_columns(blocks, start, width, parts=1):
    count, rows, _ = blocks.shape
    each = width // parts
    if each % 128 or start % width or rows % 96:
        picked = blocks[:, :, start : start + width].reshape(count, rows, parts, each)
        whole = jnp.moveaxis(picked, 0, 2).astype(F32).reshape(rows, parts, count * each)
        return whole.reshape(rows, count * each) if parts == 1 else whole
    step = 96

    def kernel(in_ref, out_ref):
        if parts == 1:
            out_ref[...] = in_ref[...].astype(F32)
        else:
            for i in range(parts):
                out_ref[:, i, :] = in_ref[:, i * each : (i + 1) * each].astype(F32)

    shape = (rows, count * each) if parts == 1 else (rows, parts, count * each)
    block = (step, each) if parts == 1 else (step, parts, each)
    place = (lambda r, c: (r, c)) if parts == 1 else (lambda r, c: (r, 0, c))
    return pl.pallas_call(
        kernel,
        out_shape=jax.ShapeDtypeStruct(shape, F32),
        grid=(rows // step, count),
        in_specs=[pl.BlockSpec((None, step, width), lambda r, c: (c, r, start // width))],
        out_specs=pl.BlockSpec(block, place),
        compiler_params=pltpu.CompilerParams(vmem_limit_bytes=32 << 20),
    )(blocks)


def cols(values, start, width):
    return lax.dynamic_slice_in_dim(values, start, width, axis=values.ndim - 1)


def on_device(
    tokens,
    segments,
    stretch_order,
    norm_gains,
    query_proj,
    keyval_proj,
    attn_proj,
    ffn_in,
    ffn_out,
    cotangent,
):
    seq_count, _, _, half_dev, width = tokens.shape
    fsdp_count = lax.axis_size("fsdp")
    ctx_count = lax.axis_size("ctx")
    tp_count = lax.axis_size("tp")
    fsdp_at, ctx_at, tp_at = (lax.axis_index(name) for name in ("fsdp", "ctx", "tp"))
    row_count = seq_count * 2 * half_dev
    own_count = row_count // tp_count
    group_rows = own_count * tp_count * ctx_count
    assert seq_count == tp_count

    head_count = query_proj.shape[1] // HEAD_DIM
    group = head_count // (keyval_proj.shape[2] // HEAD_DIM)
    repeat = ctx_count // head_count
    assert repeat >= 1 and repeat * head_count == ctx_count
    sharers = group * repeat
    head_at = ctx_at // repeat
    kv_at = ctx_at // sharers
    share_at = ctx_at % sharers
    q_width = HEAD_DIM // repeat
    kv_width = 2 * HEAD_DIM // sharers
    q_own = (ctx_at % repeat) * q_width
    kv_own = share_at * kv_width
    ff_width = ffn_out.shape[1] // ctx_count
    ff_at = ctx_at * ff_width

    half_stretch = half_dev * fsdp_count
    length = 2 * ctx_count * half_stretch
    slot = jnp.arange(ctx_count) == ctx_at
    paired = jnp.sum(jnp.where(slot, stretch_order, 0))
    block = jnp.stack([paired, 2 * ctx_count - 1 - paired])
    position = block[:, None] * half_stretch + fsdp_at * half_dev + jnp.arange(half_dev)
    marks = segments.reshape(seq_count, 2, half_dev) * length + position[None]
    slots = -(-ctx_count // 8) * 8
    own_slot = jnp.arange(slots)[:, None] == ctx_at
    placed = jnp.where(own_slot, marks.reshape(1, -1), 0).astype(F32)
    mark_count = placed.shape[1]
    placed = jnp.tile(placed, (ctx_count, pl.cdiv(512, mark_count)))
    marks = lax.psum_scatter(placed, "ctx", scatter_dimension=0, tiled=True)
    marks = marks[:ctx_count, :mark_count].astype(jnp.int32)
    marks = marks.reshape(ctx_count, seq_count, 2 * half_dev).transpose(1, 0, 2)
    marks = xor_order(marks, ctx_at, 1).reshape(seq_count, 1, -1)
    marks = jnp.concatenate(gather_xor(marks, "fsdp"), axis=1)
    marks = jnp.where(tp_at == 0, marks, jnp.flip(marks, 0))
    query_mark = marks[:, 0]
    key_mark = marks.reshape(seq_count, -1)
    query_first = query_mark - lax.rem(query_mark, length)
    allowed = (key_mark[:, None, :] <= query_mark[:, :, None]) & (
        key_mark[:, None, :] >= query_first[:, :, None]
    )

    kv_part = cols(keyval_proj, kv_at * HEAD_DIM, HEAD_DIM)
    att_part = jnp.concatenate(
        [
            cols(query_proj, head_at * HEAD_DIM, HEAD_DIM),
            kv_part[:, 0],
            kv_part[:, 1],
            cols(attn_proj, head_at * HEAD_DIM, HEAD_DIM),
        ],
        axis=1,
    )
    w_first, w_second = gather_weights(att_part, fsdp_at)
    w_attn = w_second[:, HEAD_DIM:]
    in_part = cols(ffn_in, ff_at, ff_width)
    ffn_part = jnp.concatenate(
        [in_part[:, 0], in_part[:, 1], cols(ffn_out, ff_at, ff_width)], axis=1
    )
    w_ffn = lax.all_gather(ffn_part, "fsdp", axis=0, tiled=True)
    w_in, w_out = w_ffn[:, : 2 * ff_width], w_ffn[:, 2 * ff_width :]

    gain_pre, gain_post, gain_ffn, gain_last = (norm_gains[i] for i in range(4))
    row_at = tp_at * own_count
    tok_in = lax.dynamic_slice_in_dim(
        tokens.reshape(row_count, width), row_at, own_count, 0
    ).astype(F32)
    cot_in = lax.dynamic_slice_in_dim(
        cotangent.reshape(row_count, width), row_at, own_count, 0
    ).astype(F32)

    xnorm_own = (tok_in * rms_factor(tok_in) * gain_pre).astype(BF16)
    xnorm = gather_rows(xnorm_own)
    w_qkv = jnp.concatenate([w_first, w_second[:, :HEAD_DIM]], axis=1)
    qkv = dot_nn(xnorm, w_qkv).astype(BF16)
    query = qkv[:, :HEAD_DIM].reshape(seq_count, -1, HEAD_DIM)
    kv_own_rows = qkv[:, HEAD_DIM:].reshape(seq_count, -1, 2 * HEAD_DIM)
    kv_all = jnp.concatenate(gather_xor(kv_own_rows, "fsdp"), axis=1)
    keys, vals = kv_all[:, :, :HEAD_DIM], kv_all[:, :, HEAD_DIM:]
    raw_scores = jnp.einsum("sqe,ske->sqk", query, keys, preferred_element_type=F32)
    capped = SOFT_CAP * jnp.tanh(raw_scores * (HEAD_DIM ** (-0.5) / SOFT_CAP))
    expo = jnp.where(allowed, jnp.exp(capped), 0.0)
    denom = jnp.sum(expo, axis=-1, keepdims=True)
    mixture = jnp.einsum("sqk,ske->sqe", expo.astype(BF16), vals, preferred_element_type=F32)
    attended_seq = (mixture / denom).astype(BF16)
    lse = jnp.log(denom)
    attended = attended_seq.reshape(group_rows, HEAD_DIM)
    attended_own = attended if repeat == 1 else cols(attended, q_own, q_width)
    w_attn_own = w_attn if repeat == 1 else cols(w_attn, q_own, q_width)
    branch = scatter_rows(dot_nt(attended_own, w_attn_own))

    hidden = tok_in + branch * rms_factor(branch) * gain_post
    hnorm = gather_rows((hidden * rms_factor(hidden) * gain_ffn).astype(BF16))
    both = dot_nn(hnorm, w_in)
    gate, up = both[:, :ff_width], both[:, ff_width:]
    gelu_vals, gelu_slope = gelu_parts(gate)
    middle = (gelu_vals * up).astype(BF16)
    ffout = scatter_rows(dot_nt(middle, w_out))
    result = (hidden + ffout * rms_factor(ffout) * gain_last).astype(BF16)

    grad_ff, grad_last_gain = norm_back(cot_in, ffout, gain_last)
    grad_ffb = gather_rows(grad_ff.astype(BF16))
    grad_mid = dot_nn(grad_ffb, w_out)
    grad_both = jnp.concatenate(
        [grad_mid * up * gelu_slope, grad_mid * gelu_vals], axis=1
    ).astype(BF16)

    def weight_grad(left, right):
        return lax.psum_scatter(
            dot_tn(left, right).astype(BF16), "fsdp", scatter_dimension=0, tiled=True
        )

    def spread(part):
        return lax.all_gather(part, "ctx", axis=0, tiled=False)

    part_out = weight_grad(grad_ffb, middle)
    part_in = weight_grad(hnorm, grad_both)

    grad_hn = scatter_rows(dot_nt(grad_both, w_in))
    grad_hid_n, grad_ffn_gain = norm_back(grad_hn, hidden, gain_ffn)
    grad_hidden = cot_in + grad_hid_n
    grad_branch, grad_post_gain = norm_back(grad_hidden, branch, gain_post)
    grad_branchb = gather_rows(grad_branch.astype(BF16))
    grad_branchb = after(grad_branchb, part_out)
    all_out = spread(part_out)

    grad_attended = dot_nn(grad_branchb, w_attn).astype(BF16)
    grad_att_seq = grad_attended.reshape(seq_count, -1, HEAD_DIM)
    delta = jnp.sum(
        grad_att_seq.astype(F32) * attended_seq.astype(F32), axis=-1, keepdims=True
    )
    prob = jnp.where(allowed, jnp.exp(capped - lse), 0.0)
    grad_prob = jnp.einsum("sqe,ske->sqk", grad_att_seq, vals, preferred_element_type=F32)
    ratio = capped / SOFT_CAP
    grad_raw = prob * (grad_prob - delta) * (1.0 - ratio * ratio) * HEAD_DIM ** (-0.5)
    raw_half = grad_raw.astype(BF16)
    prob_half = prob.astype(BF16)
    grad_q = jnp.einsum("sqk,ske->sqe", raw_half, keys, preferred_element_type=F32).astype(BF16)
    grad_k = jnp.einsum("sqk,sqe->ske", raw_half, query, preferred_element_type=F32)
    grad_v = jnp.einsum("sqk,sqe->ske", prob_half, grad_att_seq, preferred_element_type=F32)
    pieces = jnp.stack([grad_k, grad_v])
    pieces = pieces.reshape(2, *grad_k.shape[:2], sharers // 2, kv_width)
    pieces = pieces.transpose(0, 3, 1, 2, 4).reshape(sharers, *grad_k.shape[:2], kv_width)
    kv_term = lax.dynamic_index_in_dim(pieces, share_at, 0, keepdims=False)
    for j in range(repeat, sharers, repeat):
        sent = lax.dynamic_index_in_dim(pieces, share_at ^ j, 0, keepdims=False).astype(BF16)
        by_ctx = sent.reshape(seq_count, fsdp_count, ctx_count, -1, kv_width)
        sent = xor_order(by_ctx, j, 2).reshape(sent.shape)
        kv_term = kv_term + swap(sent, "ctx", j).astype(F32)
    kv_term = kv_term.reshape(seq_count, fsdp_count, -1, kv_width)
    grad_kv = scatter_xor([kv_term[:, j] for j in range(fsdp_count)], "fsdp").astype(BF16).reshape(group_rows, kv_width)
    grad_q = grad_q.reshape(group_rows, HEAD_DIM)
    grad_q_own = grad_q if repeat == 1 else cols(grad_q, q_own, q_width)
    grad_qkv = jnp.concatenate([grad_q_own, grad_kv], axis=1)
    grad_qkv = after(grad_qkv, part_in, all_out)
    all_in = spread(part_in)
    w_q_own = w_qkv[:, :HEAD_DIM] if repeat == 1 else cols(w_qkv, q_own, q_width)
    w_qkv_own = jnp.concatenate([w_q_own, cols(w_qkv, HEAD_DIM + kv_own, kv_width)], axis=1)
    grad_xnorm = scatter_rows(dot_nt(grad_qkv, w_qkv_own))
    grad_x_n, grad_pre_gain = norm_back(grad_xnorm, tok_in, gain_pre)
    grad_tokens_own = grad_hidden + grad_x_n

    att_term = jnp.concatenate(
        [dot_tn(xnorm, grad_qkv).astype(BF16), dot_tn(grad_branchb, attended_own).astype(BF16)],
        axis=1,
    )
    part_att = lax.psum_scatter(att_term, "fsdp", scatter_dimension=0, tiled=True)
    all_att = spread(after(part_att, all_in))

    grad_gains = sum_all(
        jnp.stack([grad_pre_gain, grad_post_gain, grad_ffn_gain, grad_last_gain], axis=0)
    )
    result = both_cores(result, tp_at)
    grad_tokens = both_cores(grad_tokens_own, tp_at)

    grad_ffn_in = spread_columns(all_in, 0, 2 * ff_width, 2)
    grad_ffn_out = spread_columns(all_out, 0, ff_width)
    grad_query = spread_columns(all_att, 0, q_width)
    grad_attn = spread_columns(all_att, q_width + kv_width, q_width)
    own_width = all_att.shape[1]
    grad_keyval = (
        all_att[:, :, q_width : q_width + kv_width]
        .reshape(ctx_count // sharers, 2, sharers // 2, own_width, kv_width)
        .transpose(3, 1, 0, 2, 4)
        .astype(F32)
        .reshape(own_width, 2, -1)
    )
    return (
        result.reshape(tokens.shape),
        grad_tokens.reshape(tokens.shape),
        grad_gains,
        grad_query,
        grad_keyval,
        grad_attn,
        grad_ffn_in,
        grad_ffn_out,
    )


def solution(mesh):
    placed = (
        P(None, None, "ctx", "fsdp", None),
        P(None, None, "ctx", "fsdp"),
        P(),
        P(),
        P("fsdp", "tp"),
        P("fsdp", None, "tp"),
        P("fsdp", "tp"),
        P("fsdp", None, "tp"),
        P("fsdp", "tp"),
        P(None, None, "ctx", "fsdp", None),
    )
    return jax.shard_map(
        on_device,
        mesh=mesh,
        in_specs=placed,
        out_specs=(
            P(None, None, "ctx", "fsdp", None),
            P(None, None, "ctx", "fsdp", None),
            P(),
            P("fsdp", "tp"),
            P("fsdp", None, "tp"),
            P("fsdp", "tp"),
            P("fsdp", None, "tp"),
            P("fsdp", "tp"),
        ),
        check_vma=False,
    )
```
